128 devices in a mesh: gx: 8 (over y, x_hi), gy: 16 (over x_lo, z, core).
Axes of the slice: x: 4 (x_hi: 2, x_lo: 2; x = x_hi * 2 + x_lo), y: 4, z: 4, core: 2. Of those that a mesh axis runs over, the one named last changes fastest.
Arguments:
- charges: float32 [512, 256, 128], P('gx', 'gy'), may hold values from -6 to 6
- kernel_fine: bfloat16 [9, 9, 9], replicated, may hold values from -0.21875 to 0.21875
- kernel_mid: bfloat16 [9, 9, 9], replicated, may hold values from -0.109375 to 0.109375
- kernel_coarse: bfloat16 [9, 9, 9], replicated, may hold values from -0.0546875 to 0.0546875
Outputs:
- potential: float32 [512, 256, 128], P('gx', 'gy')
The draws below stay inside these ranges and needn't reach their ends.
All inputs are finite; a program needn't handle non-finite values.
Results may differ from the reference program's by a relative error of at most 0.0028.
Values may be sent and summed in bfloat16 or wider, within the bound.
A program may use at most 128 MiB of HBM per device.

```python
import math
import jax
import jax.numpy as jnp
from jax import lax

CZ = 128
GRID_X = 512
GRID_Y = 256


def level_of(stream_key, extent, split, smallest, high):
    loudness, own = 1.0, jax.random.fold_in(stream_key, 6)
    for axis_at, blocks in split:
        heights = jnp.exp(jax.random.uniform(jax.random.fold_in(own, axis_at), (blocks,), jnp.float32, smallest / len(split), high / len(split)))
        loudness = loudness * jnp.repeat(heights, extent[axis_at] // blocks).reshape([-1 if axis == axis_at else 1 for axis in range(len(extent))])
    return loudness


def bell_draw(rng, dims, width, limit, pieces=(), held_as=jnp.bfloat16):
    drawn = jax.random.normal(rng, dims, jnp.float32) * width
    if len(pieces) > 0:
        drawn = level_of(rng, dims, pieces, -0.22, 0.18) * drawn
    return jnp.clip(drawn, min=-limit, max=limit).astype(held_as)


def setup_inputs(seed: int = 0) -> dict:
    seeds = jax.random.split(jax.random.key(seed), 5)
    return {
        "charges": bell_draw(seeds[0], (GRID_X, GRID_Y, CZ), 1.0, 6.0, ((0, 8), (1, 16)), jnp.float32),
        "kernel_fine": bell_draw(seeds[1], (9, 9, 9), 729 ** -0.5, 0.21875),
        "kernel_mid": bell_draw(seeds[2], (9, 9, 9), 2916 ** -0.5, 0.109375),
        "kernel_coarse": bell_draw(seeds[3], (9, 9, 9), 11664 ** -0.5, 0.0546875),
    }


restrict_taps = ((-3, -0.0625), (-1, 0.5625), (0, 1.0), (1, 0.5625), (3, -0.0625))


def restrict_matrix(fine_cells):
    fine_index = lax.broadcasted_iota(jnp.int32, (fine_cells, fine_cells // 2), 0)
    coarse_index = lax.broadcasted_iota(jnp.int32, (fine_cells, fine_cells // 2), 1)
    spacing = fine_index - 2 * coarse_index
    matrix = jnp.zeros((fine_cells, fine_cells // 2), jnp.float32)
    for offset, factor in restrict_taps:
        matrix = matrix + jnp.where(spacing == offset, jnp.float32(factor), jnp.float32(0.0))
    return matrix


def restrict_axis(padded, axis, coarse_cells):
    result = None
    for offset, factor in restrict_taps:
        sliced = lax.slice_in_dim(padded, 3 + offset, 3 + offset + 2 * coarse_cells - 1, 2, axis)
        result = factor * sliced if result is None else result + factor * sliced
    return result


def restrict(padded):
    along_x = restrict_axis(padded, 0, (padded.shape[0] - 6) // 2)
    along_y = restrict_axis(along_x, 1, (padded.shape[1] - 6) // 2)
    matrix = restrict_matrix(along_y.shape[2])
    return jnp.einsum("xyz,zc->xyc", along_y, matrix, precision=lax.Precision.HIGHEST)


def prolong_axis(padded, axis, coarse_cells):
    def shifted(first_index):
        return lax.slice_in_dim(padded, first_index, first_index + coarse_cells, 1, axis)
    even_cells = shifted(2)
    odd_cells = 0.5625 * (shifted(2) + shifted(3)) - 0.0625 * (shifted(1) + shifted(4))
    paired = jnp.stack([even_cells, odd_cells], axis=axis + 1)
    new_shape = list(even_cells.shape)
    new_shape[axis] = 2 * coarse_cells
    return paired.reshape(new_shape)


def prolong(padded):
    along_x = prolong_axis(padded, 0, padded.shape[0] - 4)
    along_y = prolong_axis(along_x, 1, padded.shape[1] - 4)
    matrix = restrict_matrix(2 * along_y.shape[2])
    return jnp.einsum("xyc,zc->xyz", along_y, matrix, precision=lax.Precision.HIGHEST)


def grid_convolve(field, kernel):
    cells_x, cells_y, cells_z = field.shape
    slab_rows = math.gcd(cells_x, 64)
    size_x = slab_rows + 16
    size_y = ((cells_y + 8 + 63) // 64) * 64
    size_z = ((cells_z + 8 + 63) // 64) * 64
    fft_shape = (size_x, size_y, size_z)
    flipped = kernel[::-1, ::-1, ::-1]
    kernel_hat = jnp.fft.rfftn(flipped, s=fft_shape)
    padded = jnp.pad(field, ((4, 4), (0, 0), (0, 0)))

    def one_slab(first_row):
        slab_input = lax.dynamic_slice_in_dim(padded, first_row, slab_rows + 8, 0)
        product = jnp.fft.irfftn(jnp.fft.rfftn(slab_input, s=fft_shape) * kernel_hat, s=fft_shape)
        return product[8:8 + slab_rows, 4:4 + cells_y, 4:4 + cells_z]

    slab_starts = jnp.arange(cells_x // slab_rows, dtype=jnp.int32) * slab_rows
    slab_results = lax.map(one_slab, slab_starts)
    return slab_results.reshape(cells_x, cells_y, cells_z)


def rounded_copy(field):
    narrow = lax.optimization_barrier(field.astype(jnp.bfloat16))
    return narrow.astype(jnp.float32)


def reference(charges, kernel_fine, kernel_mid, kernel_coarse):
    fine_potential = grid_convolve(rounded_copy(charges), kernel_fine.astype(jnp.float32))
    mid_charges = restrict(jnp.pad(charges, ((3, 3), (3, 3), (0, 0))))
    mid_potential = grid_convolve(rounded_copy(mid_charges), kernel_mid.astype(jnp.float32))
    coarse_charges = restrict(jnp.pad(mid_charges, ((3, 3), (3, 3), (0, 0))))
    coarse_potential = grid_convolve(rounded_copy(coarse_charges), kernel_coarse.astype(jnp.float32))
    mid_total = mid_potential + prolong(jnp.pad(coarse_potential, ((2, 2), (2, 2), (0, 0))))
    return fine_potential + prolong(jnp.pad(mid_total, ((2, 2), (2, 2), (0, 0))))
```

```python
import functools

import jax
import jax.numpy as jnp
import numpy as np
from jax import lax
from jax.experimental import pallas as pl
from jax.experimental.pallas import tpu as pltpu
from jax.sharding import PartitionSpec as P

bf16, f32 = jnp.bfloat16, jnp.float32
MESH = pl.DeviceIdType.MESH
TAPS = {-3: -0.0625, -1: 0.5625, 0: 1.0, 1: 0.5625, 3: -0.0625}
LEVELS = ((128, 1, 9), (64, 2, 10), (32, 4, 12))
NEAR = ((0, -1), (0, 1), (-1, 0), (1, 0), (-1, -1), (-1, 1), (1, -1), (1, 1))
FAR = tuple((i, j) for i in (-1, 0, 1) for j in (-2, -1, 0, 1, 2) if (i, j) != (0, 0))


def taps_matrix(fine, coarse):
    spacing = np.asarray(fine)[:, None] - 2 * np.asarray(coarse)[None, :]
    matrix = np.zeros(spacing.shape, np.float32)
    for offset, factor in TAPS.items():
        matrix[spacing == offset] = factor
    return matrix


def constants():
    rz = taps_matrix(range(128), range(64))
    block_z = np.kron(np.eye(2, dtype=np.float32), rz)
    rz_mid = taps_matrix(range(64), range(32))
    to_coarse = np.kron(taps_matrix(range(-4, 10), range(4)), rz_mid)
    to_mid = np.concatenate([to_coarse[128 * m:128 * m + 128].T for m in range(7)])
    pieces = {}

    def wide(matrix):
        return np.pad(matrix, ((0, 0), (0, 128 - matrix.shape[1])))

    mid_rows = [r - 8 for r in range(48)]
    pieces["block_z"] = block_z
    pieces["spread_z"] = np.concatenate([block_z.T[:, :128], block_z.T[:, 128:]])
    pieces["to_coarse"] = to_coarse
    pieces["to_mid"] = to_mid
    rx = taps_matrix(range(64), mid_rows).T
    pieces["rx"] = np.concatenate([rx, rx], axis=1)
    rc = taps_matrix(mid_rows, range(16)).T
    pieces["rc"] = wide(np.concatenate([rc, rc], axis=1))
    pc = taps_matrix([o - 1 for o in range(48)], [i - 2 for i in range(32)])
    pc[35:] = 0.0
    pieces["pc"] = wide(np.concatenate([pc, pc], axis=1))
    px = taps_matrix(range(64), [o - 1 for o in range(48)])
    px[:, 35:] = 0.0
    pieces["px"] = wide(np.concatenate([px, px], axis=1))
    at, rows = {}, 0
    for name, piece in pieces.items():
        at[name] = (rows, piece.shape[0])
        rows += piece.shape[0]
    return np.concatenate(list(pieces.values())), at


TABLE, AT = constants()


def high_low(value):
    high = value.astype(bf16)
    return high, (value - high.astype(f32)).astype(bf16)


def dot(a, b):
    return jnp.dot(a, b, preferred_element_type=f32)


def toeplitz(kernel, base, table, level, first):
    cells, blocks, rows = LEVELS[level]
    width = 128 * blocks
    tap = lax.broadcasted_iota(jnp.int32, (9, width), 0)
    lane = lax.broadcasted_iota(jnp.int32, (9, width), 1)
    target = cells * (lane // 128) + 4 - tap
    place = jnp.where((lane - target) % 128 == 0, 1.0, 0.0).astype(bf16)
    base[...] = jnp.zeros_like(base)
    for dx in range(9):
        placed = dot(kernel[dx], place)
        for b in range(blocks):
            base[dx, b:b + 9, :] += placed[:, 128 * b:128 * b + 128]
    row = lax.broadcasted_iota(jnp.int32, (8, 128), 0)
    column = lax.broadcasted_iota(jnp.int32, (8, 128), 1) % cells
    top = jnp.abs(row - column) <= 4
    bottom = jnp.abs(row + cells - 8 - column) <= 4
    for dx in range(9):
        for e in range(rows):
            line = jnp.broadcast_to(base[dx, e:e + 1, :], (cells, 128))
            rolled = pltpu.roll(line, 0, 1, stride=1, stride_axis=0)
            band = jnp.concatenate(
                [jnp.where(top, rolled[:8], 0.0), rolled[8:cells - 8], jnp.where(bottom, rolled[cells - 8:], 0.0)], axis=0)
            table[dx, first + e * cells:first + (e + 1) * cells, :] = band.astype(bf16)
    if first:
        end = first + rows * cells
        for dx in range(9):
            table[dx, 0:first, :] = jnp.zeros((first, 128), bf16)
            table[dx, end:end + first, :] = jnp.zeros((first, 128), bf16)


def wide_table(table, dx, depth):
    return jnp.concatenate([table[dx, 128:128 + depth, :], table[dx, 0:depth, :]], axis=1)


def body(sizes, c_hbm, kf, km, kc, const_hbm, out,
         c, const, field, base_f, base_m, base_c, tab_f, tab_m, tab_c,
         v_in, v_ed, fine, y_s, y_r, x_s, x_r, k_s, k_r, m_s, my_r, mx_r, mk_r,
         mid, coarse_s, coarse_r, coarse, u_ref,
         load_sem, fs_sem, fr_sem, ms_sem, mr_sem, cs_sem, cr_sem):
    gx, gy = lax.axis_index("gx"), lax.axis_index("gy")
    nx, ny = sizes

    def device(i, j):
        return (lax.rem(gx + i + nx, nx), lax.rem(gy + j + ny, ny))

    def from_inside(i, j):
        x, y = gx - i, gy - j
        return (x >= 0) & (x < nx) & (y >= 0) & (y < ny)

    def inside_columns(matrix, period, first, end):
        place = lax.broadcasted_iota(jnp.int32, matrix.shape, 1) % period
        keep = ((place >= first) | (gx > 0)) & ((place < end) | (gx < nx - 1))
        return jnp.where(keep, matrix.astype(f32), 0.0).astype(bf16)

    def inside_y(value, place):
        if place == 0:
            return value
        return jnp.where(gy > 0 if place < 0 else gy < ny - 1, value, 0.0)

    load_c = pltpu.make_async_copy(c_hbm, c, load_sem.at[0])
    load_k = pltpu.make_async_copy(const_hbm, const, load_sem.at[1])
    load_c.start()
    load_k.start()
    barrier = pltpu.get_barrier_semaphore()
    for i, j in FAR:
        pl.semaphore_signal(barrier, inc=1, device_id=device(i, j), device_id_type=MESH)

    def table(name, width=128):
        start, rows = AT[name]
        return const[start:start + rows, 0:width]

    toeplitz(kf, base_f, tab_f, 0, 128)
    load_c.wait()
    for y in range(16):
        for b in range(8):
            field[4 + y, 8 + 8 * b:16 + 8 * b, :] = c[pl.ds(128 * b + y, 8, stride=16), :]
    for d, y0 in ((0, 0), (1, 12)):
        for y in range(4):
            y_s[d, y] = field[4 + y0 + y, 8:72, :].astype(bf16)
    for d, x0 in ((0, 0), (1, 60)):
        for x in range(4):
            x_s[d, x] = c[16 * (x0 + x):16 * (x0 + x) + 16, :].astype(bf16)
    for n, (i, j) in enumerate(NEAR[4:]):
        r0, y0 = (8 if i < 0 else 64), (4 if j < 0 else 16)
        for h in range(2):
            k_s[n, 16 * h:16 * h + 16, :] = jnp.concatenate(
                [field[y0 + 2 * h, r0:r0 + 8, :], field[y0 + 2 * h + 1, r0:r0 + 8, :]], axis=0).astype(bf16)

    load_k.wait()

    def along_y(row):
        total = None
        for offset, factor in TAPS.items():
            y = 2 * row + offset
            if 0 <= y < 16:
                term = factor * field[4 + y, 8:72, :]
                total = term if total is None else total + term
        return jnp.zeros((64, 128), f32) if total is None else total

    highs, lows = [], []
    for p in range(-1, 5):
        he, le = high_low(along_y(2 * p))
        ho, lo = high_low(along_y(2 * p + 1))
        highs.append(jnp.concatenate([he, ho], axis=1))
        lows.append(jnp.concatenate([le, lo], axis=1))
    shares = dot(jnp.concatenate(highs, axis=0), table("block_z")) + dot(jnp.concatenate(lows, axis=0), table("block_z"))
    split = []
    for p in range(6):
        high, low = high_low(shares[64 * p:64 * p + 64])
        split.append(jnp.concatenate([high, low], axis=0))
    share = dot(table("rx"), jnp.concatenate(split, axis=1))
    mid[...] = jnp.zeros_like(mid)
    mid[0:48, 256:1024] = share
    m_s[...] = share.astype(bf16)

    pl.semaphore_wait(barrier, len(FAR))
    sends = []

    def send(source, target, send_sem, recv_sem, i, j):
        copy = pltpu.make_async_remote_copy(
            src_ref=source, dst_ref=target, send_sem=send_sem, recv_sem=recv_sem,
            device_id=device(i, j), device_id_type=MESH)
        copy.start()
        return copy

    fine_copies, mid_copies = [], []
    for n, (i, j) in enumerate(NEAR):
        if i == 0:
            pair = (m_s.at[:, 0:512] if j < 0 else m_s.at[:, 256:768], my_r.at[n])
        elif j == 0:
            pair = (m_s.at[0:16, :] if i < 0 else m_s.at[32:48, :], mx_r.at[n - 2])
        else:
            rows = pl.ds(0, 16) if i < 0 else pl.ds(32, 16)
            columns = pl.ds(0, 512) if j < 0 else pl.ds(256, 512)
            pair = (m_s.at[rows, columns], mk_r.at[n - 4])
        mid_copies.append(send(*pair, ms_sem.at[n], mr_sem.at[n], i, j))
        if i == 0:
            pair = (y_s.at[n], y_r.at[n])
        elif j == 0:
            pair = (x_s.at[n - 2], x_r.at[n - 2])
        else:
            pair = (k_s.at[n - 4], k_r.at[n - 4])
        fine_copies.append(send(*pair, fs_sem.at[n], fr_sem.at[n], i, j))

    toeplitz(km, base_m, tab_m, 1, 128)
    toeplitz(kc, base_c, tab_c, 2, 0)

    def fill_inside(rows):
        for dx in range(9):
            for y in rows:
                v_in[dx, y] = field[y, 12 + dx:60 + dx, :].astype(bf16)

    def fine_inside(pairs):
        weights = jnp.concatenate([wide_table(tab_f, dx, 1280) for dx in range(9)], axis=0)
        left = jnp.concatenate(
            [jnp.concatenate([v_in[dx, 2 * q + k] for dx in range(9) for k in range(10)], axis=1) for q in pairs], axis=0)
        result = dot(left, weights)
        for n, q in enumerate(pairs):
            for k in range(2):
                fine[2 * q + k, 8:56, :] = result[48 * n:48 * n + 48, 128 * k:128 * k + 128]

    fill_inside(range(4, 20))
    fine_inside((2, 3, 4, 5))

    for n, (i, j) in enumerate(NEAR):
        mid_copies[n].wait_recv()
    for n, (i, j) in enumerate(NEAR):
        inside = from_inside(i, j)
        got = my_r[n] if i == 0 else mx_r[n - 2] if j == 0 else mk_r[n - 4]
        got = jnp.where(inside, got.astype(f32), 0.0)
        r0, rows = (0, 48) if i == 0 else (32, 16) if i < 0 else (0, 16)
        l0, lanes = (256, 768) if j == 0 else (768, 512) if j < 0 else (0, 512)
        mid[r0:r0 + rows, l0:l0 + lanes] += got
    @pl.when(gx == 0)
    def _():
        mid[0:8, :] = jnp.zeros((8, 1280), f32)

    @pl.when(gx == nx - 1)
    def _():
        mid[40:48, :] = jnp.zeros((8, 1280), f32)

    @pl.when(gy == 0)
    def _():
        mid[0:48, 0:384] = jnp.zeros((48, 384), f32)

    @pl.when(gy == ny - 1)
    def _():
        mid[0:48, 896:1280] = jnp.zeros((48, 384), f32)

    high, low = high_low(mid[0:48, 128:1024])
    shrunk = dot(table("rc", 96), jnp.concatenate([high, low], axis=0))
    high, low = high_low(shrunk)
    own = dot(jnp.concatenate([high, low], axis=0), table("to_coarse"))
    own = (own[0:16] + own[16:32]).astype(bf16)
    coarse_s[...] = own
    coarse_copies = [send(coarse_s, coarse_r.at[n], cs_sem.at[n], cr_sem.at[n], i, j) for n, (i, j) in enumerate(FAR)]

    for n in range(2):
        fine_copies[n].wait_recv()
        inside = from_inside(*NEAR[n])
        for y in range(4):
            field[(20 if n == 0 else 0) + y, 8:72, :] = jnp.where(inside, y_r[n, y].astype(f32), 0.0)
    fill_inside((0, 1, 2, 3, 20, 21, 22, 23))
    fine_inside((0, 1, 6, 7))
    for n in range(2, 4):
        fine_copies[n].wait_recv()
        inside = from_inside(*NEAR[n])
        for x in range(4):
            got = jnp.where(inside, x_r[n - 2, x].astype(f32), 0.0)
            for y in range(2):
                for k in range(8):
                    row = (72 if n == 2 else 4) + x
                    field[4 + 8 * y + k, row:row + 1, :] = got[8 * y + k:8 * y + k + 1, :]
    for n in range(4, 8):
        fine_copies[n].wait_recv()
        i, j = NEAR[n]
        inside = from_inside(i, j)
        r0, y0 = (72 if i < 0 else 0), (20 if j < 0 else 0)
        for h in range(2):
            got = jnp.where(inside, k_r[n - 4, 16 * h:16 * h + 16, :].astype(f32), 0.0)
            field[y0 + 2 * h, r0:r0 + 8, :] = got[0:8]
            field[y0 + 2 * h + 1, r0:r0 + 8, :] = got[8:16]
    for dx in range(9):
        for y in range(24):
            v_ed[dx, y] = jnp.concatenate(
                [field[y, 4 + dx:12 + dx, :], field[y, 60 + dx:68 + dx, :]], axis=0).astype(bf16)
    weights = jnp.concatenate([wide_table(tab_f, dx, 1280) for dx in range(9)], axis=0)
    left = jnp.concatenate(
        [jnp.concatenate([v_ed[dx, 2 * q + k] for dx in range(9) for k in range(10)], axis=1) for q in range(8)], axis=0)
    result = dot(left, weights)
    for q in range(8):
        for k in range(2):
            piece = result[16 * q:16 * q + 16, 128 * k:128 * k + 128]
            fine[2 * q + k, 0:8, :] = piece[0:8]
            fine[2 * q + k, 56:64, :] = piece[8:16]

    weights = jnp.concatenate([wide_table(tab_m, dx, 768) for dx in range(9)], axis=0)
    shifted = [mid[3 + dx:51 + dx, :].astype(bf16) for dx in range(9)]
    left = jnp.concatenate(
        [jnp.concatenate([shifted[dx][:, 256 * g:256 * g + 768] for dx in range(9)], axis=1) for g in range(3)], axis=0)
    mid_potential = dot(left, weights)

    coarse[48:56, :] = jnp.zeros((8, 640), f32)
    coarse[16:32, 256:384] = own.astype(f32)
    for n, (i, j) in enumerate(FAR):
        coarse_copies[n].wait_recv()
        coarse[16 - 16 * i:32 - 16 * i, 256 - 128 * j:384 - 128 * j] = jnp.where(
            from_inside(i, j), coarse_r[n].astype(f32), 0.0)
    weights = jnp.concatenate([tab_c[dx] for dx in range(9)], axis=0)
    shifted = [coarse[10 + dx:42 + dx, :].astype(bf16) for dx in range(9)]
    left = jnp.concatenate(
        [jnp.concatenate([shifted[dx][:, 128 * q:128 * q + 384] for dx in range(9)], axis=1) for q in range(3)], axis=0)
    coarse_potential = dot(left, weights)
    split = []
    for q in range(3):
        high, low = high_low(inside_y(coarse_potential[32 * q:32 * q + 32], q - 1))
        split.append(jnp.concatenate([high, low], axis=0))
    spread = dot(inside_columns(table("pc", 64), 32, 2, 18), jnp.concatenate(split, axis=1))
    high, low = high_low(spread)
    spread = jnp.concatenate([high, low], axis=0)
    to_mid = AT["to_mid"][0]
    split = []
    for p in range(-1, 5):
        g, h = (p + 1) // 2, (p + 1) % 2
        total = mid_potential[48 * g:48 * g + 48, 128 * h:128 * h + 128]
        for q in (-1, 0, 1):
            m = p - 4 * q + 2
            if 0 <= m < 7:
                part = dot(spread[:, 128 * (q + 1):128 * (q + 1) + 128], const[to_mid + 128 * m:to_mid + 128 * m + 128, :])
                total = total + (part[0:48] + part[48:96])
        high, low = high_low(inside_y(total, -1 if p < 0 else 1 if p > 3 else 0))
        split.append(jnp.concatenate([high, low], axis=0))
    along_x = dot(inside_columns(table("px", 96), 48, 1, 33), jnp.concatenate(split, axis=1))
    highs, lows = [], []
    for p in range(6):
        high, low = high_low(along_x[:, 128 * p:128 * p + 128])
        highs.append(high)
        lows.append(low)
    spread_z = AT["spread_z"][0]
    weights = jnp.concatenate([const[spread_z:spread_z + 128, :], const[spread_z + 128:spread_z + 256, :]], axis=1)
    along_z = dot(jnp.concatenate(highs, axis=0), weights) + dot(jnp.concatenate(lows, axis=0), weights)
    for p in range(6):
        for k in range(2):
            u_ref[2 * p + k] = along_z[64 * p:64 * p + 64, 128 * k:128 * k + 128]
    for b in range(8):
        even = fine[2 * b] + u_ref[b + 2]
        odd = fine[2 * b + 1] + (0.5625 * (u_ref[b + 2] + u_ref[b + 3]) - 0.0625 * (u_ref[b + 1] + u_ref[b + 4]))
        for x in range(8):
            out[pl.ds(128 * x + 2 * b, 8, stride=16), :] = even[8 * x:8 * x + 8]
            out[pl.ds(128 * x + 2 * b + 1, 8, stride=16), :] = odd[8 * x:8 * x + 8]
    for copy in fine_copies + mid_copies + coarse_copies:
        copy.wait_send()


def solution(mesh):
    sizes = (mesh.shape["gx"], mesh.shape["gy"])
    vmem, dma = pltpu.VMEM, pltpu.SemaphoreType.DMA
    in_vmem, anywhere = pl.BlockSpec(memory_space=pltpu.VMEM), pl.BlockSpec(memory_space=pl.ANY)

    def local(charges, kernel_fine, kernel_mid, kernel_coarse):
        call = pl.pallas_call(
            functools.partial(body, sizes),
            out_shape=jax.ShapeDtypeStruct((1024, 128), f32),
            in_specs=[anywhere, in_vmem, in_vmem, in_vmem, anywhere],
            out_specs=in_vmem,
            scratch_shapes=[
                vmem((1024, 128), f32), vmem(TABLE.shape, bf16), vmem((24, 80, 128), f32),
                vmem((9, 16, 128), f32), vmem((9, 16, 128), f32), vmem((9, 16, 128), f32),
                vmem((9, 1408, 128), bf16), vmem((9, 896, 128), bf16), vmem((9, 384, 128), bf16),
                vmem((9, 24, 48, 128), bf16), vmem((9, 24, 16, 128), bf16), vmem((16, 64, 128), f32),
                vmem((2, 4, 64, 128), bf16), vmem((2, 4, 64, 128), bf16),
                vmem((2, 4, 16, 128), bf16), vmem((2, 4, 16, 128), bf16),
                vmem((4, 32, 128), bf16), vmem((4, 32, 128), bf16),
                vmem((48, 768), bf16), vmem((2, 48, 512), bf16), vmem((2, 16, 768), bf16), vmem((4, 16, 512), bf16),
                vmem((64, 1280), f32), vmem((16, 128), bf16), vmem((14, 16, 128), bf16), vmem((56, 640), f32),
                vmem((12, 64, 128), f32),
                dma((2,)), dma((8,)), dma((8,)), dma((8,)), dma((8,)), dma((14,)), dma((14,)),
            ],
            compiler_params=pltpu.CompilerParams(
                collective_id=0, has_side_effects=True, vmem_limit_bytes=56 * 2**20),
            name="multilevel",
        )
        table = jnp.asarray(TABLE, bf16)
        return call(charges.reshape(1024, 128), kernel_fine, kernel_mid, kernel_coarse, table).reshape(64, 16, 128)

    placed = (P("gx", "gy", None), P(), P(), P())
    return jax.shard_map(local, mesh=mesh, in_specs=placed, out_specs=P("gx", "gy", None), check_vma=False)
```

```python
import functools

import jax
import jax.numpy as jnp
import numpy as np
from jax import lax
from jax.experimental import pallas as pl
from jax.experimental.pallas import tpu as pltpu
from jax.sharding import PartitionSpec as P

bf16, f32 = jnp.bfloat16, jnp.float32
MESH = pl.DeviceIdType.MESH
TAPS = {-3: -0.0625, -1: 0.5625, 0: 1.0, 1: 0.5625, 3: -0.0625}
LEVELS = ((128, 1, 9), (64, 2, 10), (32, 4, 12))
NEAR = ((0, -1), (0, 1), (-1, 0), (1, 0), (-1, -1), (-1, 1), (1, -1), (1, 1))
FAR = tuple((i, j) for i in (-1, 0, 1) for j in range(-3, 4) if (i, j) != (0, 0))
QUADS = {-3: (0, 1), -2: (0, 2), -1: (0, 3), 0: (0, 3), 1: (0, 3), 2: (1, 3), 3: (2, 3)}


def taps_matrix(fine, coarse):
    spacing = np.asarray(fine)[:, None] - 2 * np.asarray(coarse)[None, :]
    matrix = np.zeros(spacing.shape, np.float32)
    for offset, factor in TAPS.items():
        matrix[spacing == offset] = factor
    return matrix


def constants():
    rz = taps_matrix(range(128), range(64))
    block_z = np.kron(np.eye(2, dtype=np.float32), rz)
    rz_mid = taps_matrix(range(64), range(32))
    to_coarse = np.kron(taps_matrix(range(-4, 10), range(4)), rz_mid)
    to_mid = np.concatenate([to_coarse[128 * m:128 * m + 128].T for m in range(7)])
    pieces = {}

    def wide(matrix):
        return np.pad(matrix, ((0, 0), (0, 128 - matrix.shape[1])))

    mid_rows = [r - 8 for r in range(48)]
    pieces["block_z"] = block_z
    pieces["spread_z"] = np.concatenate([block_z.T[:, :128], block_z.T[:, 128:]])
    pieces["to_coarse"] = to_coarse
    pieces["to_mid"] = to_mid
    rx = taps_matrix(range(64), mid_rows).T
    pieces["rx"] = np.concatenate([rx, rx], axis=1)
    rc = taps_matrix(mid_rows, [r - 6 for r in range(32)]).T
    pieces["rc"] = wide(np.concatenate([rc, rc], axis=1))
    pc = taps_matrix([o - 1 for o in range(48)], [i - 2 for i in range(32)])
    pc[35:] = 0.0
    pieces["pc"] = wide(np.concatenate([pc, pc], axis=1))
    px = taps_matrix(range(64), [o - 1 for o in range(48)])
    px[:, 35:] = 0.0
    pieces["px"] = wide(np.concatenate([px, px], axis=1))
    at, rows = {}, 0
    for name, piece in pieces.items():
        at[name] = (rows, piece.shape[0])
        rows += piece.shape[0]
    return np.concatenate(list(pieces.values())), at


TABLE, AT = constants()


def high_low(value):
    high = value.astype(bf16)
    return high, (value - high.astype(f32)).astype(bf16)


def dot(a, b):
    return jnp.dot(a, b, preferred_element_type=f32)


def toeplitz(kernel, base, table, level, first):
    cells, blocks, rows = LEVELS[level]
    width = 128 * blocks
    tap = lax.broadcasted_iota(jnp.int32, (9, width), 0)
    lane = lax.broadcasted_iota(jnp.int32, (9, width), 1)
    target = cells * (lane // 128) + 4 - tap
    place = jnp.where((lane - target) % 128 == 0, 1.0, 0.0).astype(bf16)
    base[...] = jnp.zeros_like(base)
    for dx in range(9):
        placed = dot(kernel[dx], place)
        for b in range(blocks):
            base[dx, b:b + 9, :] += placed[:, 128 * b:128 * b + 128]
    row = lax.broadcasted_iota(jnp.int32, (8, 128), 0)
    column = lax.broadcasted_iota(jnp.int32, (8, 128), 1) % cells
    top = jnp.abs(row - column) <= 4
    bottom = jnp.abs(row + cells - 8 - column) <= 4
    for dx in range(9):
        for e in range(rows):
            line = jnp.broadcast_to(base[dx, e:e + 1, :], (cells, 128))
            rolled = pltpu.roll(line, 0, 1, stride=1, stride_axis=0)
            band = jnp.concatenate(
                [jnp.where(top, rolled[:8], 0.0), rolled[8:cells - 8], jnp.where(bottom, rolled[cells - 8:], 0.0)], axis=0)
            table[dx, first + e * cells:first + (e + 1) * cells, :] = band.astype(bf16)
    if first:
        end = first + rows * cells
        for dx in range(9):
            table[dx, 0:first, :] = jnp.zeros((first, 128), bf16)
            table[dx, end:end + first, :] = jnp.zeros((first, 128), bf16)


def wide_table(table, dx, depth):
    return jnp.concatenate([table[dx, 128:128 + depth, :], table[dx, 0:depth, :]], axis=1)


def body(sizes, c_hbm, kf_hbm, km_hbm, kc_hbm, const_hbm, out,
         c, const, kf, km, kc, field, base_f, base_m, base_c, tab_f, tab_m, tab_c,
         v_in, v_ed, fine, y_s, y_r, x_s, x_r, k_s, k_r, m_s, my_r, mx_r, mk_r,
         mid, coarse_s, coarse_r, coarse, u_ref,
         load_sem, fs_sem, fr_sem, ms_sem, mr_sem, cs_sem, cr_sem):
    gx, gy = lax.axis_index("gx"), lax.axis_index("gy")
    nx, ny = sizes

    def device(i, j):
        return (lax.rem(gx + i + nx, nx), lax.rem(gy + j + ny, ny))

    def from_inside(i, j):
        x, y = gx - i, gy - j
        return (x >= 0) & (x < nx) & (y >= 0) & (y < ny)

    def inside_x(matrix, axis, period, first, end):
        place = lax.broadcasted_iota(jnp.int32, matrix.shape, axis) % period
        keep = ((place >= first) | (gx > 0)) & ((place < end) | (gx < nx - 1))
        return jnp.where(keep, matrix.astype(f32), 0.0).astype(bf16)

    def inside_y(value, place):
        if place == 0:
            return value
        return jnp.where(gy > 0 if place < 0 else gy < ny - 1, value, 0.0)

    load_c = pltpu.make_async_copy(c_hbm, c, load_sem.at[0])
    load_k = pltpu.make_async_copy(const_hbm, const, load_sem.at[1])
    load_s = [pltpu.make_async_copy(source, target, load_sem.at[2 + n])
              for n, (source, target) in enumerate(((kf_hbm, kf), (km_hbm, km), (kc_hbm, kc)))]
    load_c.start()
    load_k.start()
    for load in load_s:
        load.start()
    barrier = pltpu.get_barrier_semaphore()
    for i, j in FAR:
        pl.semaphore_signal(barrier, inc=1, device_id=device(i, j), device_id_type=MESH)

    def table(name, width=128):
        start, rows = AT[name]
        return const[start:start + rows, 0:width]

    load_c.wait()
    for y in range(16):
        for b in range(8):
            field[4 + y, 8 + 8 * b:16 + 8 * b, :] = c[pl.ds(128 * b + y, 8, stride=16), :]
    for d, y0 in ((0, 0), (1, 12)):
        for y in range(4):
            y_s[d, y] = field[4 + y0 + y, 8:72, :].astype(bf16)
    for d, x0 in ((0, 0), (1, 60)):
        for x in range(4):
            x_s[d, x] = c[16 * (x0 + x):16 * (x0 + x) + 16, :].astype(bf16)
    for n, (i, j) in enumerate(NEAR[4:]):
        r0, y0 = (8 if i < 0 else 64), (4 if j < 0 else 16)
        for h in range(2):
            k_s[n, 16 * h:16 * h + 16, :] = jnp.concatenate(
                [field[y0 + 2 * h, r0:r0 + 8, :], field[y0 + 2 * h + 1, r0:r0 + 8, :]], axis=0).astype(bf16)

    load_k.wait()

    def along_y(row):
        total = None
        for offset, factor in TAPS.items():
            y = 2 * row + offset
            if 0 <= y < 16:
                term = factor * field[4 + y, 8:72, :]
                total = term if total is None else total + term
        return jnp.zeros((64, 128), f32) if total is None else total

    highs, lows = [], []
    for p in range(-1, 5):
        he, le = high_low(along_y(2 * p))
        ho, lo = high_low(along_y(2 * p + 1))
        highs.append(jnp.concatenate([he, ho], axis=1))
        lows.append(jnp.concatenate([le, lo], axis=1))
    shares = dot(jnp.concatenate(highs, axis=0), table("block_z")) + dot(jnp.concatenate(lows, axis=0), table("block_z"))
    split = []
    for p in range(6):
        high, low = high_low(inside_y(shares[64 * p:64 * p + 64], (p == 5) - (p == 0)))
        split.append(jnp.concatenate([high, low], axis=0))
    share = dot(inside_x(table("rx"), 0, 48, 8, 40), jnp.concatenate(split, axis=1))
    mid[...] = jnp.zeros_like(mid)
    mid[0:48, 256:1024] = share
    m_s[...] = share.astype(bf16)
    high, low = high_low(share)
    high, low = high_low(dot(inside_x(table("rc", 96), 0, 32, 6, 22), jnp.concatenate([high, low], axis=0)))
    both = jnp.concatenate([high, low], axis=0)
    weights = AT["to_coarse"][0]
    coarse[...] = jnp.zeros_like(coarse)
    for q, (p0, p1, m0) in enumerate(((0, 2, 5), (0, 6, 1), (3, 6, 0))):
        part = dot(both[:, 128 * p0:128 * p1], const[weights + 128 * m0:weights + 128 * (m0 + p1 - p0), :])
        part = inside_y(part[0:32] + part[32:64], q - 1)
        coarse[0:32, 128 * q + 128:128 * q + 256] = part
        coarse_s[:, 128 * q:128 * q + 128] = part.astype(bf16)

    pl.semaphore_wait(barrier, len(FAR))
    sends = []

    def send(source, target, send_sem, recv_sem, i, j):
        copy = pltpu.make_async_remote_copy(
            src_ref=source, dst_ref=target, send_sem=send_sem, recv_sem=recv_sem,
            device_id=device(i, j), device_id_type=MESH)
        copy.start()
        return copy

    fine_copies, mid_copies, coarse_copies = [], [], []
    for n, (i, j) in enumerate(FAR):
        q0, q1 = QUADS[j]
        rows = pl.ds(0, 32) if i == 0 else pl.ds(0, 16) if i < 0 else pl.ds(16, 16)
        columns = pl.ds(0, 128 * (q1 - q0))
        coarse_copies.append(send(
            coarse_s.at[rows, pl.ds(128 * q0, 128 * (q1 - q0))], coarse_r.at[n, rows, columns], cs_sem.at[n], cr_sem.at[n], i, j))
    for n, (i, j) in enumerate(NEAR):
        if i == 0:
            pair = (m_s.at[:, 0:512] if j < 0 else m_s.at[:, 256:768], my_r.at[n])
        elif j == 0:
            pair = (m_s.at[0:16, :] if i < 0 else m_s.at[32:48, :], mx_r.at[n - 2])
        else:
            rows = pl.ds(0, 16) if i < 0 else pl.ds(32, 16)
            columns = pl.ds(0, 512) if j < 0 else pl.ds(256, 512)
            pair = (m_s.at[rows, columns], mk_r.at[n - 4])
        mid_copies.append(send(*pair, ms_sem.at[n], mr_sem.at[n], i, j))
        if i == 0:
            pair = (y_s.at[n], y_r.at[n])
        elif j == 0:
            pair = (x_s.at[n - 2], x_r.at[n - 2])
        else:
            pair = (k_s.at[n - 4], k_r.at[n - 4])
        fine_copies.append(send(*pair, fs_sem.at[n], fr_sem.at[n], i, j))

    for load in load_s:
        load.wait()
    toeplitz(kf, base_f, tab_f, 0, 128)
    toeplitz(km, base_m, tab_m, 1, 128)
    toeplitz(kc, base_c, tab_c, 2, 0)

    def fill_inside(rows):
        for dx in range(9):
            for y in rows:
                v_in[dx, y] = field[y, 12 + dx:60 + dx, :].astype(bf16)

    def fine_inside(pairs):
        weights = jnp.concatenate([wide_table(tab_f, dx, 1280) for dx in range(9)], axis=0)
        left = jnp.concatenate(
            [jnp.concatenate([v_in[dx, 2 * q + k] for dx in range(9) for k in range(10)], axis=1) for q in pairs], axis=0)
        result = dot(left, weights)
        for n, q in enumerate(pairs):
            for k in range(2):
                fine[2 * q + k, 8:56, :] = result[48 * n:48 * n + 48, 128 * k:128 * k + 128]

    fill_inside(range(4, 20))
    fine_inside((2, 3, 4, 5))

    for n, (i, j) in enumerate(NEAR):
        mid_copies[n].wait_recv()
    for n, (i, j) in enumerate(NEAR):
        inside = from_inside(i, j)
        got = my_r[n] if i == 0 else mx_r[n - 2] if j == 0 else mk_r[n - 4]
        got = jnp.where(inside, got.astype(f32), 0.0)
        r0, rows = (0, 48) if i == 0 else (32, 16) if i < 0 else (0, 16)
        l0, lanes = (256, 768) if j == 0 else (768, 512) if j < 0 else (0, 512)
        mid[r0:r0 + rows, l0:l0 + lanes] += got
    for n in range(2):
        fine_copies[n].wait_recv()
        inside = from_inside(*NEAR[n])
        for y in range(4):
            field[(20 if n == 0 else 0) + y, 8:72, :] = jnp.where(inside, y_r[n, y].astype(f32), 0.0)
    fill_inside((0, 1, 2, 3, 20, 21, 22, 23))
    fine_inside((0, 1, 6, 7))
    for n in range(2, 4):
        fine_copies[n].wait_recv()
        inside = from_inside(*NEAR[n])
        for x in range(4):
            got = jnp.where(inside, x_r[n - 2, x].astype(f32), 0.0)
            for y in range(2):
                for k in range(8):
                    row = (72 if n == 2 else 4) + x
                    field[4 + 8 * y + k, row:row + 1, :] = got[8 * y + k:8 * y + k + 1, :]
    for n in range(4, 8):
        fine_copies[n].wait_recv()
        i, j = NEAR[n]
        inside = from_inside(i, j)
        r0, y0 = (72 if i < 0 else 0), (20 if j < 0 else 0)
        for h in range(2):
            got = jnp.where(inside, k_r[n - 4, 16 * h:16 * h + 16, :].astype(f32), 0.0)
            field[y0 + 2 * h, r0:r0 + 8, :] = got[0:8]
            field[y0 + 2 * h + 1, r0:r0 + 8, :] = got[8:16]
    for dx in range(9):
        for y in range(24):
            v_ed[dx, y] = jnp.concatenate(
                [field[y, 4 + dx:12 + dx, :], field[y, 60 + dx:68 + dx, :]], axis=0).astype(bf16)
    weights = jnp.concatenate([wide_table(tab_f, dx, 1280) for dx in range(9)], axis=0)
    left = jnp.concatenate(
        [jnp.concatenate([v_ed[dx, 2 * q + k] for dx in range(9) for k in range(10)], axis=1) for q in range(8)], axis=0)
    result = dot(left, weights)
    for q in range(8):
        for k in range(2):
            piece = result[16 * q:16 * q + 16, 128 * k:128 * k + 128]
            fine[2 * q + k, 0:8, :] = piece[0:8]
            fine[2 * q + k, 56:64, :] = piece[8:16]

    weights = jnp.concatenate([wide_table(tab_m, dx, 768) for dx in range(9)], axis=0)
    shifted = [mid[3 + dx:51 + dx, :].astype(bf16) for dx in range(9)]
    left = jnp.concatenate(
        [jnp.concatenate([shifted[dx][:, 256 * g:256 * g + 768] for dx in range(9)], axis=1) for g in range(3)], axis=0)
    mid_potential = dot(left, weights)

    for n, (i, j) in enumerate(FAR):
        coarse_copies[n].wait_recv()
    for n, (i, j) in enumerate(FAR):
        q0, q1 = QUADS[j]
        r0, rows = (0, 32) if i == 0 else (16, 16) if i < 0 else (0, 16)
        t0 = 0 if i <= 0 else 16
        l0, lanes = 128 * (q0 + 1 - j), 128 * (q1 - q0)
        got = coarse_r[n, t0:t0 + rows, 0:lanes].astype(f32)
        coarse[r0:r0 + rows, l0:l0 + lanes] += jnp.where(from_inside(i, j), got, 0.0)

    weights = jnp.concatenate([tab_c[dx] for dx in range(9)], axis=0)
    shifted = [coarse[dx:32 + dx, :].astype(bf16) for dx in range(9)]
    left = jnp.concatenate(
        [jnp.concatenate([shifted[dx][:, 128 * q:128 * q + 384] for dx in range(9)], axis=1) for q in range(3)], axis=0)
    coarse_potential = dot(left, weights)
    split = []
    for q in range(3):
        high, low = high_low(inside_y(coarse_potential[32 * q:32 * q + 32], q - 1))
        split.append(jnp.concatenate([high, low], axis=0))
    spread = dot(inside_x(table("pc", 64), 1, 32, 2, 18), jnp.concatenate(split, axis=1))
    high, low = high_low(spread)
    spread = jnp.concatenate([high, low], axis=0)
    to_mid = AT["to_mid"][0]
    split = []
    for p in range(-1, 5):
        g, h = (p + 1) // 2, (p + 1) % 2
        total = mid_potential[48 * g:48 * g + 48, 128 * h:128 * h + 128]
        for q in (-1, 0, 1):
            m = p - 4 * q + 2
            if 0 <= m < 7:
                part = dot(spread[:, 128 * (q + 1):128 * (q + 1) + 128], const[to_mid + 128 * m:to_mid + 128 * m + 128, :])
                total = total + (part[0:48] + part[48:96])
        high, low = high_low(inside_y(total, -1 if p < 0 else 1 if p > 3 else 0))
        split.append(jnp.concatenate([high, low], axis=0))
    along_x = dot(inside_x(table("px", 96), 1, 48, 1, 33), jnp.concatenate(split, axis=1))
    highs, lows = [], []
    for p in range(6):
        high, low = high_low(along_x[:, 128 * p:128 * p + 128])
        highs.append(high)
        lows.append(low)
    spread_z = AT["spread_z"][0]
    weights = jnp.concatenate([const[spread_z:spread_z + 128, :], const[spread_z + 128:spread_z + 256, :]], axis=1)
    along_z = dot(jnp.concatenate(highs, axis=0), weights) + dot(jnp.concatenate(lows, axis=0), weights)
    for p in range(6):
        for k in range(2):
            u_ref[2 * p + k] = along_z[64 * p:64 * p + 64, 128 * k:128 * k + 128]
    for b in range(8):
        even = fine[2 * b] + u_ref[b + 2]
        odd = fine[2 * b + 1] + (0.5625 * (u_ref[b + 2] + u_ref[b + 3]) - 0.0625 * (u_ref[b + 1] + u_ref[b + 4]))
        for x in range(8):
            out[pl.ds(128 * x + 2 * b, 8, stride=16), :] = even[8 * x:8 * x + 8]
            out[pl.ds(128 * x + 2 * b + 1, 8, stride=16), :] = odd[8 * x:8 * x + 8]
    for copy in fine_copies + mid_copies + coarse_copies:
        copy.wait_send()


def solution(mesh):
    sizes = (mesh.shape["gx"], mesh.shape["gy"])
    vmem, dma = pltpu.VMEM, pltpu.SemaphoreType.DMA
    in_vmem, in_hbm = pl.BlockSpec(memory_space=pltpu.VMEM), pl.BlockSpec(memory_space=pltpu.HBM)

    def local(charges, kernel_fine, kernel_mid, kernel_coarse):
        call = pl.pallas_call(
            functools.partial(body, sizes),
            out_shape=jax.ShapeDtypeStruct((1024, 128), f32),
            in_specs=[in_hbm] * 5,
            out_specs=in_vmem,
            scratch_shapes=[
                vmem((1024, 128), f32), vmem(TABLE.shape, bf16),
                vmem((9, 9, 9), bf16), vmem((9, 9, 9), bf16), vmem((9, 9, 9), bf16), vmem((24, 80, 128), f32),
                vmem((9, 16, 128), f32), vmem((9, 16, 128), f32), vmem((9, 16, 128), f32),
                vmem((9, 1408, 128), bf16), vmem((9, 896, 128), bf16), vmem((9, 384, 128), bf16),
                vmem((9, 24, 48, 128), bf16), vmem((9, 24, 16, 128), bf16), vmem((16, 64, 128), f32),
                vmem((2, 4, 64, 128), bf16), vmem((2, 4, 64, 128), bf16),
                vmem((2, 4, 16, 128), bf16), vmem((2, 4, 16, 128), bf16),
                vmem((4, 32, 128), bf16), vmem((4, 32, 128), bf16),
                vmem((48, 768), bf16), vmem((2, 48, 512), bf16), vmem((2, 16, 768), bf16), vmem((4, 16, 512), bf16),
                vmem((64, 1280), f32), vmem((32, 384), bf16), vmem((20, 32, 384), bf16), vmem((40, 640), f32),
                vmem((12, 64, 128), f32),
                dma((5,)), dma((8,)), dma((8,)), dma((8,)), dma((8,)), dma((20,)), dma((20,)),
            ],
            compiler_params=pltpu.CompilerParams(
                collective_id=0, has_side_effects=True, vmem_limit_bytes=56 * 2**20),
            name="multilevel",
        )
        table = jnp.asarray(TABLE, bf16)
        return call(charges.reshape(1024, 128), kernel_fine, kernel_mid, kernel_coarse, table).reshape(64, 16, 128)

    placed = (P("gx", "gy", None), P(), P(), P())
    return jax.shard_map(local, mesh=mesh, in_specs=placed, out_specs=P("gx", "gy", None), check_vma=False)
```

```python
import functools

import jax
import jax.numpy as jnp
import numpy as np
from jax import lax
from jax.experimental import pallas as pl
from jax.experimental.pallas import tpu as pltpu
from jax.sharding import PartitionSpec as P

bf16, f32 = jnp.bfloat16, jnp.float32
MESH = pl.DeviceIdType.MESH
TAPS = {-3: -0.0625, -1: 0.5625, 0: 1.0, 1: 0.5625, 3: -0.0625}
LEVELS = ((128, 1, 9), (64, 2, 10), (32, 4, 12))
NEAR = ((0, -1), (0, 1), (-1, 0), (1, 0), (-1, -1), (-1, 1), (1, -1), (1, 1))
FAR = tuple((i, j) for i in (-1, 0, 1) for j in range(-3, 4) if (i, j) != (0, 0))
QUADS = {-3: (0, 1), -2: (0, 2), -1: (0, 3), 0: (0, 3), 1: (0, 3), 2: (1, 3), 3: (2, 3)}


def taps_matrix(fine, coarse):
    spacing = np.asarray(fine)[:, None] - 2 * np.asarray(coarse)[None, :]
    matrix = np.zeros(spacing.shape, np.float32)
    for offset, factor in TAPS.items():
        matrix[spacing == offset] = factor
    return matrix


def constants():
    rz = taps_matrix(range(128), range(64))
    block_z = np.kron(np.eye(2, dtype=np.float32), rz)
    rz_mid = taps_matrix(range(64), range(32))
    to_coarse = np.kron(taps_matrix(range(-4, 10), range(4)), rz_mid)
    to_mid = np.concatenate([to_coarse[128 * m:128 * m + 128].T for m in range(7)])
    pieces = {}

    def wide(matrix):
        return np.pad(matrix, ((0, 0), (0, 128 - matrix.shape[1])))

    mid_rows = [r - 8 for r in range(48)]
    pieces["block_z"] = block_z
    pieces["spread_z"] = np.concatenate([block_z.T[:, :128], block_z.T[:, 128:]])
    pieces["to_coarse"] = to_coarse
    pieces["to_mid"] = to_mid
    rx = taps_matrix(range(64), mid_rows).T
    pieces["rx"] = np.concatenate([rx, rx], axis=1)
    rc = taps_matrix(mid_rows, [r - 6 for r in range(32)]).T
    pieces["rc"] = wide(np.concatenate([rc, rc], axis=1))
    pc = taps_matrix([o - 1 for o in range(48)], [i - 2 for i in range(32)])
    pc[35:] = 0.0
    pieces["pc"] = wide(np.concatenate([pc, pc], axis=1))
    px = taps_matrix(range(64), [o - 1 for o in range(48)])
    px[:, 35:] = 0.0
    pieces["px"] = wide(np.concatenate([px, px], axis=1))
    at, rows = {}, 0
    for name, piece in pieces.items():
        at[name] = (rows, piece.shape[0])
        rows += piece.shape[0]
    return np.concatenate(list(pieces.values())), at


TABLE, AT = constants()


def high_low(value):
    high = value.astype(bf16)
    return high, (value - high.astype(f32)).astype(bf16)


def dot(a, b):
    return jnp.dot(a, b, preferred_element_type=f32)


def toeplitz(kernel, base, table, level, first):
    cells, blocks, rows = LEVELS[level]
    width = 128 * blocks
    tap = lax.broadcasted_iota(jnp.int32, (9, width), 0)
    lane = lax.broadcasted_iota(jnp.int32, (9, width), 1)
    target = cells * (lane // 128) + 4 - tap
    place = jnp.where((lane - target) % 128 == 0, 1.0, 0.0).astype(bf16)
    base[...] = jnp.zeros_like(base)
    for dx in range(9):
        placed = dot(kernel[dx], place)
        for b in range(blocks):
            base[dx, b:b + 9, :] += placed[:, 128 * b:128 * b + 128]
    row = lax.broadcasted_iota(jnp.int32, (8, 128), 0)
    column = lax.broadcasted_iota(jnp.int32, (8, 128), 1) % cells
    top = jnp.abs(row - column) <= 4
    bottom = jnp.abs(row + cells - 8 - column) <= 4
    for dx in range(9):
        for e in range(rows):
            line = jnp.broadcast_to(base[dx, e:e + 1, :], (cells, 128))
            rolled = pltpu.roll(line, 0, 1, stride=1, stride_axis=0)
            band = jnp.concatenate(
                [jnp.where(top, rolled[:8], 0.0), rolled[8:cells - 8], jnp.where(bottom, rolled[cells - 8:], 0.0)], axis=0)
            table[dx, first + e * cells:first + (e + 1) * cells, :] = band.astype(bf16)
    if first:
        end = first + rows * cells
        for dx in range(9):
            table[dx, 0:first, :] = jnp.zeros((first, 128), bf16)
            table[dx, end:end + first, :] = jnp.zeros((first, 128), bf16)


def wide_table(table, dx, depth):
    return jnp.concatenate([table[dx, 128:128 + depth, :], table[dx, 0:depth, :]], axis=1)


def body(sizes, c_hbm, kf_hbm, km_hbm, kc_hbm, const_hbm, out,
         c, const, kf, km, kc, field, base_f, base_m, base_c, tab_f, tab_m, tab_c,
         v_in, v_ed, fine, y_s, y_r, x_s, x_r, k_s, k_r, m_s, my_r, mx_r, mk_r,
         mid, coarse_s, coarse_r, coarse, u_ref,
         load_sem, fs_sem, fr_sem, ms_sem, mr_sem, cs_sem, cr_sem):
    gx, gy = lax.axis_index("gx"), lax.axis_index("gy")
    nx, ny = sizes

    def wrapped(place, size):
        return jnp.where(place < 0, place + size, jnp.where(place >= size, place - size, place))

    along_gx = {i: wrapped(gx + i, nx) for i in (-1, 0, 1)}
    along_gy = {j: wrapped(gy + j, ny) for j in range(-3, 4)}

    def device(i, j):
        return (along_gx[i], along_gy[j])

    def from_inside(i, j):
        x, y = gx - i, gy - j
        return (x >= 0) & (x < nx) & (y >= 0) & (y < ny)

    def inside_x(matrix, axis, period, first, end):
        place = lax.broadcasted_iota(jnp.int32, matrix.shape, axis) % period
        keep = ((place >= first) | (gx > 0)) & ((place < end) | (gx < nx - 1))
        return jnp.where(keep, matrix.astype(f32), 0.0).astype(bf16)

    def inside_y(value, place):
        if place == 0:
            return value
        return jnp.where(gy > 0 if place < 0 else gy < ny - 1, value, 0.0)

    load_c = pltpu.make_async_copy(c_hbm, c, load_sem.at[0])
    load_k = pltpu.make_async_copy(const_hbm, const, load_sem.at[1])
    load_s = [pltpu.make_async_copy(source, target, load_sem.at[2 + n])
              for n, (source, target) in enumerate(((kf_hbm, kf), (km_hbm, km), (kc_hbm, kc)))]
    load_c.start()
    load_k.start()
    for load in load_s:
        load.start()
    barrier = pltpu.get_barrier_semaphore()
    for i, j in FAR:
        pl.semaphore_signal(barrier, inc=1, device_id=device(i, j), device_id_type=MESH)

    def table(name, width=128):
        start, rows = AT[name]
        return const[start:start + rows, 0:width]

    load_c.wait()
    for y in range(16):
        for b in range(8):
            field[4 + y, 8 + 8 * b:16 + 8 * b, :] = c[pl.ds(128 * b + y, 8, stride=16), :]
    for d, y0 in ((0, 0), (1, 12)):
        for y in range(4):
            y_s[d, y] = field[4 + y0 + y, 8:72, :].astype(bf16)
    for d, x0 in ((0, 0), (1, 60)):
        for x in range(4):
            x_s[d, x] = c[16 * (x0 + x):16 * (x0 + x) + 16, :].astype(bf16)
    for n, (i, j) in enumerate(NEAR[4:]):
        r0, y0 = (8 if i < 0 else 64), (4 if j < 0 else 16)
        for h in range(2):
            k_s[n, 16 * h:16 * h + 16, :] = jnp.concatenate(
                [field[y0 + 2 * h, r0:r0 + 8, :], field[y0 + 2 * h + 1, r0:r0 + 8, :]], axis=0).astype(bf16)

    load_k.wait()

    def along_y(row):
        total = None
        for offset, factor in TAPS.items():
            y = 2 * row + offset
            if 0 <= y < 16:
                term = factor * field[4 + y, 8:72, :]
                total = term if total is None else total + term
        return jnp.zeros((64, 128), f32) if total is None else total

    highs, lows = [], []
    for p in range(-1, 5):
        he, le = high_low(along_y(2 * p))
        ho, lo = high_low(along_y(2 * p + 1))
        highs.append(jnp.concatenate([he, ho], axis=1))
        lows.append(jnp.concatenate([le, lo], axis=1))
    shares = dot(jnp.concatenate(highs, axis=0), table("block_z")) + dot(jnp.concatenate(lows, axis=0), table("block_z"))
    split = []
    for p in range(6):
        high, low = high_low(inside_y(shares[64 * p:64 * p + 64], (p == 5) - (p == 0)))
        split.append(jnp.concatenate([high, low], axis=0))
    share = dot(inside_x(table("rx"), 0, 48, 8, 40), jnp.concatenate(split, axis=1))
    mid[...] = jnp.zeros_like(mid)
    mid[0:48, 256:1024] = share
    m_s[...] = share.astype(bf16)
    high, low = high_low(share)
    high, low = high_low(dot(inside_x(table("rc", 96), 0, 32, 6, 22), jnp.concatenate([high, low], axis=0)))
    both = jnp.concatenate([high, low], axis=0)
    weights = AT["to_coarse"][0]
    coarse[...] = jnp.zeros_like(coarse)
    for q, (p0, p1, m0) in enumerate(((0, 2, 5), (0, 6, 1), (3, 6, 0))):
        part = dot(both[:, 128 * p0:128 * p1], const[weights + 128 * m0:weights + 128 * (m0 + p1 - p0), :])
        part = inside_y(part[0:32] + part[32:64], q - 1)
        coarse[0:32, 128 * q + 128:128 * q + 256] = part
        coarse_s[:, 128 * q:128 * q + 128] = part.astype(bf16)

    pl.semaphore_wait(barrier, len(FAR))
    sends = []

    def send(source, target, send_sem, recv_sem, i, j):
        copy = pltpu.make_async_remote_copy(
            src_ref=source, dst_ref=target, send_sem=send_sem, recv_sem=recv_sem,
            device_id=device(i, j), device_id_type=MESH)
        copy.start()
        return copy

    fine_copies, mid_copies, coarse_copies = [], [], []
    for n, (i, j) in enumerate(NEAR):
        if i == 0:
            pair = (y_s.at[n], y_r.at[n])
        elif j == 0:
            pair = (x_s.at[n - 2], x_r.at[n - 2])
        else:
            pair = (k_s.at[n - 4], k_r.at[n - 4])
        fine_copies.append(send(*pair, fs_sem.at[n], fr_sem.at[n], i, j))
    for n, (i, j) in enumerate(NEAR):
        if i == 0:
            pair = (m_s.at[:, 0:512] if j < 0 else m_s.at[:, 256:768], my_r.at[n])
        elif j == 0:
            pair = (m_s.at[0:16, :] if i < 0 else m_s.at[32:48, :], mx_r.at[n - 2])
        else:
            rows = pl.ds(0, 16) if i < 0 else pl.ds(32, 16)
            columns = pl.ds(0, 512) if j < 0 else pl.ds(256, 512)
            pair = (m_s.at[rows, columns], mk_r.at[n - 4])
        mid_copies.append(send(*pair, ms_sem.at[n], mr_sem.at[n], i, j))
    for n, (i, j) in enumerate(FAR):
        q0, q1 = QUADS[j]
        rows = pl.ds(0, 32) if i == 0 else pl.ds(0, 16) if i < 0 else pl.ds(16, 16)
        columns = pl.ds(0, 128 * (q1 - q0))
        coarse_copies.append(send(
            coarse_s.at[rows, pl.ds(128 * q0, 128 * (q1 - q0))], coarse_r.at[n, rows, columns], cs_sem.at[n], cr_sem.at[n], i, j))

    for load in load_s:
        load.wait()
    toeplitz(kf, base_f, tab_f, 0, 128)
    toeplitz(km, base_m, tab_m, 1, 128)
    toeplitz(kc, base_c, tab_c, 2, 0)

    def fill_inside(rows):
        for dx in range(9):
            for y in rows:
                v_in[dx, y] = field[y, 12 + dx:60 + dx, :].astype(bf16)

    def fine_inside(pairs):
        weights = jnp.concatenate([wide_table(tab_f, dx, 1280) for dx in range(9)], axis=0)
        left = jnp.concatenate(
            [jnp.concatenate([v_in[dx, 2 * q + k] for dx in range(9) for k in range(10)], axis=1) for q in pairs], axis=0)
        result = dot(left, weights)
        for n, q in enumerate(pairs):
            for k in range(2):
                fine[2 * q + k, 8:56, :] = result[48 * n:48 * n + 48, 128 * k:128 * k + 128]

    fill_inside(range(4, 20))
    fine_inside((2, 3, 4, 5))

    for n in range(2):
        fine_copies[n].wait_recv()
        inside = from_inside(*NEAR[n])
        for y in range(4):
            field[(20 if n == 0 else 0) + y, 8:72, :] = jnp.where(inside, y_r[n, y].astype(f32), 0.0)
    fill_inside((0, 1, 2, 3, 20, 21, 22, 23))
    fine_inside((0, 1, 6, 7))
    for n in range(2, 4):
        fine_copies[n].wait_recv()
        inside = from_inside(*NEAR[n])
        for x in range(4):
            got = jnp.where(inside, x_r[n - 2, x].astype(f32), 0.0)
            for y in range(2):
                for k in range(8):
                    row = (72 if n == 2 else 4) + x
                    field[4 + 8 * y + k, row:row + 1, :] = got[8 * y + k:8 * y + k + 1, :]
    for n in range(4, 8):
        fine_copies[n].wait_recv()
        i, j = NEAR[n]
        inside = from_inside(i, j)
        r0, y0 = (72 if i < 0 else 0), (20 if j < 0 else 0)
        for h in range(2):
            got = jnp.where(inside, k_r[n - 4, 16 * h:16 * h + 16, :].astype(f32), 0.0)
            field[y0 + 2 * h, r0:r0 + 8, :] = got[0:8]
            field[y0 + 2 * h + 1, r0:r0 + 8, :] = got[8:16]
    for dx in range(9):
        for y in range(24):
            v_ed[dx, y] = jnp.concatenate(
                [field[y, 4 + dx:12 + dx, :], field[y, 60 + dx:68 + dx, :]], axis=0).astype(bf16)
    weights = jnp.concatenate([wide_table(tab_f, dx, 1280) for dx in range(9)], axis=0)
    left = jnp.concatenate(
        [jnp.concatenate([v_ed[dx, 2 * q + k] for dx in range(9) for k in range(10)], axis=1) for q in range(8)], axis=0)
    result = dot(left, weights)
    for q in range(8):
        for k in range(2):
            piece = result[16 * q:16 * q + 16, 128 * k:128 * k + 128]
            fine[2 * q + k, 0:8, :] = piece[0:8]
            fine[2 * q + k, 56:64, :] = piece[8:16]

    for n, (i, j) in enumerate(NEAR):
        mid_copies[n].wait_recv()
    for n, (i, j) in enumerate(NEAR):
        inside = from_inside(i, j)
        got = my_r[n] if i == 0 else mx_r[n - 2] if j == 0 else mk_r[n - 4]
        got = jnp.where(inside, got.astype(f32), 0.0)
        r0, rows = (0, 48) if i == 0 else (32, 16) if i < 0 else (0, 16)
        l0, lanes = (256, 768) if j == 0 else (768, 512) if j < 0 else (0, 512)
        mid[r0:r0 + rows, l0:l0 + lanes] += got
    weights = jnp.concatenate([wide_table(tab_m, dx, 768) for dx in range(9)], axis=0)
    shifted = [mid[3 + dx:51 + dx, :].astype(bf16) for dx in range(9)]
    left = jnp.concatenate(
        [jnp.concatenate([shifted[dx][:, 256 * g:256 * g + 768] for dx in range(9)], axis=1) for g in range(3)], axis=0)
    mid_potential = dot(left, weights)

    for n, (i, j) in enumerate(FAR):
        coarse_copies[n].wait_recv()
    for n, (i, j) in enumerate(FAR):
        q0, q1 = QUADS[j]
        r0, rows = (0, 32) if i == 0 else (16, 16) if i < 0 else (0, 16)
        t0 = 0 if i <= 0 else 16
        l0, lanes = 128 * (q0 + 1 - j), 128 * (q1 - q0)
        got = coarse_r[n, t0:t0 + rows, 0:lanes].astype(f32)
        coarse[r0:r0 + rows, l0:l0 + lanes] += jnp.where(from_inside(i, j), got, 0.0)

    weights = jnp.concatenate([tab_c[dx] for dx in range(9)], axis=0)
    shifted = [coarse[dx:32 + dx, :].astype(bf16) for dx in range(9)]
    left = jnp.concatenate(
        [jnp.concatenate([shifted[dx][:, 128 * q:128 * q + 384] for dx in range(9)], axis=1) for q in range(3)], axis=0)
    coarse_potential = dot(left, weights)
    split = []
    for q in range(3):
        high, low = high_low(inside_y(coarse_potential[32 * q:32 * q + 32], q - 1))
        split.append(jnp.concatenate([high, low], axis=0))
    spread = dot(inside_x(table("pc", 64), 1, 32, 2, 18), jnp.concatenate(split, axis=1))
    high, low = high_low(spread)
    spread = jnp.concatenate([high, low], axis=0)
    to_mid = AT["to_mid"][0]
    split = []
    for p in range(-1, 5):
        g, h = (p + 1) // 2, (p + 1) % 2
        total = mid_potential[48 * g:48 * g + 48, 128 * h:128 * h + 128]
        for q in (-1, 0, 1):
            m = p - 4 * q + 2
            if 0 <= m < 7:
                part = dot(spread[:, 128 * (q + 1):128 * (q + 1) + 128], const[to_mid + 128 * m:to_mid + 128 * m + 128, :])
                total = total + (part[0:48] + part[48:96])
        high, low = high_low(inside_y(total, -1 if p < 0 else 1 if p > 3 else 0))
        split.append(jnp.concatenate([high, low], axis=0))
    along_x = dot(inside_x(table("px", 96), 1, 48, 1, 33), jnp.concatenate(split, axis=1))
    highs, lows = [], []
    for p in range(6):
        high, low = high_low(along_x[:, 128 * p:128 * p + 128])
        highs.append(high)
        lows.append(low)
    spread_z = AT["spread_z"][0]
    weights = jnp.concatenate([const[spread_z:spread_z + 128, :], const[spread_z + 128:spread_z + 256, :]], axis=1)
    along_z = dot(jnp.concatenate(highs, axis=0), weights) + dot(jnp.concatenate(lows, axis=0), weights)
    for p in range(6):
        for k in range(2):
            u_ref[2 * p + k] = along_z[64 * p:64 * p + 64, 128 * k:128 * k + 128]
    for b in range(8):
        even = fine[2 * b] + u_ref[b + 2]
        odd = fine[2 * b + 1] + (0.5625 * (u_ref[b + 2] + u_ref[b + 3]) - 0.0625 * (u_ref[b + 1] + u_ref[b + 4]))
        for x in range(8):
            out[pl.ds(128 * x + 2 * b, 8, stride=16), :] = even[8 * x:8 * x + 8]
            out[pl.ds(128 * x + 2 * b + 1, 8, stride=16), :] = odd[8 * x:8 * x + 8]
    for copy in fine_copies + mid_copies + coarse_copies:
        copy.wait_send()


def solution(mesh):
    sizes = (mesh.shape["gx"], mesh.shape["gy"])
    vmem, dma = pltpu.VMEM, pltpu.SemaphoreType.DMA
    in_vmem, in_hbm = pl.BlockSpec(memory_space=pltpu.VMEM), pl.BlockSpec(memory_space=pltpu.HBM)

    def local(charges, kernel_fine, kernel_mid, kernel_coarse):
        call = pl.pallas_call(
            functools.partial(body, sizes),
            out_shape=jax.ShapeDtypeStruct((1024, 128), f32),
            in_specs=[in_hbm] * 5,
            out_specs=in_vmem,
            scratch_shapes=[
                vmem((1024, 128), f32), vmem(TABLE.shape, bf16),
                vmem((9, 9, 9), bf16), vmem((9, 9, 9), bf16), vmem((9, 9, 9), bf16), vmem((24, 80, 128), f32),
                vmem((9, 16, 128), f32), vmem((9, 16, 128), f32), vmem((9, 16, 128), f32),
                vmem((9, 1408, 128), bf16), vmem((9, 896, 128), bf16), vmem((9, 384, 128), bf16),
                vmem((9, 24, 48, 128), bf16), vmem((9, 24, 16, 128), bf16), vmem((16, 64, 128), f32),
                vmem((2, 4, 64, 128), bf16), vmem((2, 4, 64, 128), bf16),
                vmem((2, 4, 16, 128), bf16), vmem((2, 4, 16, 128), bf16),
                vmem((4, 32, 128), bf16), vmem((4, 32, 128), bf16),
                vmem((48, 768), bf16), vmem((2, 48, 512), bf16), vmem((2, 16, 768), bf16), vmem((4, 16, 512), bf16),
                vmem((64, 1280), f32), vmem((32, 384), bf16), vmem((20, 32, 384), bf16), vmem((40, 640), f32),
                vmem((12, 64, 128), f32),
                dma((5,)), dma((8,)), dma((8,)), dma((8,)), dma((8,)), dma((20,)), dma((20,)),
            ],
            compiler_params=pltpu.CompilerParams(
                collective_id=0, has_side_effects=True, vmem_limit_bytes=56 * 2**20),
            name="multilevel",
        )
        table = jnp.asarray(TABLE, bf16)
        return call(charges.reshape(1024, 128), kernel_fine, kernel_mid, kernel_coarse, table).reshape(64, 16, 128)

    placed = (P("gx", "gy", None), P(), P(), P())
    return jax.shard_map(local, mesh=mesh, in_specs=placed, out_specs=P("gx", "gy", None), check_vma=False)
```
